32 devices in a mesh: ctx: 8 (over z, x), head: 4 (over y, core).
Axes of the slice: x: 2, y: 2, z: 4, core: 2. Of those that a mesh axis runs over, the one named last changes fastest.
Arguments:
- queries: bfloat16 [4096, 4096], P('ctx', 'head'), may hold values from -8 to 8
- keys: bfloat16 [4096, 512], P('ctx', 'head'), may hold values from -8 to 8
- values: bfloat16 [4096, 512], P('ctx', 'head'), may hold values from -6 to 6
- distances: int32 [4, 3], P('head'), may hold values from 1 to 7, as said below
- out_weight: bfloat16 [4096, 2048], P('head'), may hold values from -0.09375 to 0.09375
- residual: bfloat16 [4096, 2048], P(('ctx', 'head')), may hold values from -6 to 6
- norm_gain: float32 [2048], replicated, may hold values from 0.25 to 1.75
- expert_gate_up: bfloat16 [32, 2048, 1536], P(('ctx', 'head')), may hold values from -0.125 to 0.125
- expert_down: bfloat16 [32, 768, 2048], P(('ctx', 'head')), may hold values from -0.21875 to 0.21875
- routes: int32 [4096, 8], P(('ctx', 'head')), may hold values from 0 to 31, all different within a row; in each aligned block of 128 rows (0 to 127, 128 to 255, ...) at most 64 rows name the same one
- route_weights: float32 [4096, 8], P(('ctx', 'head')), may hold values from 0.05 to 0.5
Outputs:
- attended: bfloat16 [4096, 2048], P(('ctx', 'head'))
- moe_out: bfloat16 [4096, 2048], P(('ctx', 'head'))
The draws below stay inside these ranges and needn't reach their ends.
Inputs may be any that keep to these rules, and one draw needn't show every extreme that they name: Each row holds 3 different distances; some row holds the distance 4096 // 1024. `routes`: among the 128 rows of one device, no expert is named by more than 64 rows.
All inputs are finite; a program needn't handle non-finite values.
Results may differ from the reference program's by a relative error of at most 0.01.
Values may be sent and summed in bfloat16 or wider, within the bound.
A program may use at most 128 MiB of HBM per device.

```python
import math
import jax
import jax.numpy as jnp
import numpy as np
from jax import lax

D = 2048
Q_HEADS = 32
KV_HEADS = 4
HD = 128
FFE = 768
TOP = 8
BLK = 128
DIST = 3
TOK_DEV = 512
TOKENS = 4096
TOK_LOC = 128
EXPERTS = 32
CAP = 64


def draw_queries(key, part):
    result = jnp.clip(jax.random.normal(jax.random.fold_in(key, 11), (TOKENS, Q_HEADS * HD), jnp.float32), -6.0, 6.0)
    return result.astype(jnp.bfloat16)


def draw_keys(key, part):
    result = jnp.clip(jax.random.normal(jax.random.fold_in(key, 12), (TOKENS, KV_HEADS * HD), jnp.float32), -6.0, 6.0)
    return result.astype(jnp.bfloat16)


def draw_distances(key, part):
    shards = TOKENS // TOK_DEV
    middle = shards // 2
    chosen = jax.random.randint(jax.random.fold_in(key, 299), (), 0, KV_HEADS)
    rows = []
    for head in range(KV_HEADS):
        others = jax.random.permutation(jax.random.fold_in(key, 300 + head), shards - 2)[:DIST] + 1
        others = jnp.where(others >= middle, others + 1, others)
        mixed_row = jnp.where((jnp.arange(DIST) == 0) & (chosen == head), middle, others)
        rows.append(mixed_row)
    return jnp.stack(rows).astype(jnp.int32)


def levels(key, shape, pieces, least, largest):
    factor_of = 1.0
    for axis_at, shards_of in pieces:
        heights = jax.random.uniform(jax.random.fold_in(jax.random.fold_in(key, 6), axis_at), (shards_of,), jnp.float32, least / len(pieces), largest / len(pieces))
        factor_of = factor_of * jnp.repeat(jnp.exp(heights), shape[axis_at] // shards_of).reshape((-1,) + (1,) * (len(shape) - 1 - axis_at))
    return factor_of


def deal_out(stream_key, own, number, rows, number_of, top, most, skew):
    ranking = jax.random.permutation(stream_key, number_of)
    heavy_load, usual = portions_of(number_of, rows * top, most, skew, True), portions_of(number_of, rows * top, most, skew, False)
    places = jnp.arange(number_of)

    def named(tallies, offset_by):
        used = int((tallies > 0).sum())
        fixed = max(1, used // 4)
        shifted = fixed + (places - fixed + offset_by * (used - fixed)) % max(1, number_of - fixed)
        return jnp.zeros((number_of,), jnp.int32).at[ranking[jnp.where(places < fixed, places, shifted)]].set(jnp.asarray(tallies, jnp.int32))

    tallies = jnp.where(number % 4 == 0, named(heavy_load, number // 4), named(usual, number - number // 4 - 1))
    mixed = jax.random.permutation(jax.random.fold_in(own, 3), number_of)
    source_of, sink = mixed[0:number_of // 2 * 2:2], mixed[1:number_of // 2 * 2:2]
    slack = jnp.minimum(tallies[source_of] - 1, most - tallies[sink]) // 2
    slack = jnp.where((source_of == ranking[0]) | (sink == ranking[0]) | (tallies[sink] == 0), 0, jnp.maximum(slack, 0))
    shifted = jax.random.randint(jax.random.fold_in(own, 4), (number_of // 2,), 0, 1 << 20) % (slack + 1)
    tallies = tallies.at[source_of].add(-shifted).at[sink].add(shifted)
    items = jnp.searchsorted(jnp.cumsum(tallies), jnp.arange(rows * top), side="right").astype(jnp.int32)
    listing = items.reshape(top, rows).T
    listing = listing[jax.random.permutation(jax.random.fold_in(own, 1), rows)]
    offset_by = jax.random.randint(jax.random.fold_in(own, 2), (rows, 1), 0, top)
    return jnp.take_along_axis(listing, (jnp.arange(top)[None, :] + offset_by) % top, axis=1)


def portions_of(number_of, total, bound, lean, full):
    weights = [(1 << 20) // math.isqrt(standing ** lean) + 1 for standing in range(1, number_of + 1)]
    largest = bound if full else min(bound, max(-(-total // number_of), total * weights[0] // sum(weights)))
    least = 1 if total - largest >= number_of - 1 else 0
    given, spare = [largest] + [least] * (number_of - 1), total - largest - least * (number_of - 1)
    while spare > 0:
        movable = [i for i in range(1, number_of) if given[i] < largest] or [i for i in range(1, number_of) if given[i] < bound]
        mass, remaining = sum([weights[i] for i in movable]), spare
        for i in movable:
            addition = min(bound - given[i], max(1, remaining * weights[i] // mass), spare)
            given[i] = given[i] + addition
            spare = spare - addition
    return np.array(given)


def scatter_about(key, shape, spread, bound, cuts=(), held_as=jnp.bfloat16):
    gain = levels(key, shape, cuts, -0.22, 0.18) if cuts else 1.0
    values = jax.random.normal(key, shape, jnp.float32) * spread * gain
    return jnp.minimum(jnp.maximum(values, -bound), bound).astype(held_as)


def setup_inputs(seed: int = 0) -> dict:
    key_list = jax.random.split(jax.random.key(seed), 12)
    queries = draw_queries(jax.random.fold_in(key_list[11], 71), 0)
    keys = draw_keys(jax.random.fold_in(key_list[11], 71), 0)
    values = scatter_about(key_list[2], (TOKENS, KV_HEADS * HD), 1.0, 6.0, ((0, 8), (1, 4)))
    distances = draw_distances(jax.random.fold_in(key_list[11], 71), 0)
    out_weight = scatter_about(key_list[4], (Q_HEADS * HD, D), (Q_HEADS * HD) ** -0.5, 0.09375, ((0, 4),))
    residual = scatter_about(key_list[5], (TOKENS, D), 1.0, 6.0, ((0, 32),))
    norm_gain = jnp.clip(1.0 + 0.15 * jax.random.normal(key_list[6], (D,), jnp.float32), 0.25, 1.75)
    expert_gate_up = scatter_about(key_list[7], (EXPERTS, D, 2 * FFE), D ** -0.5, 0.125, ((0, 32),))
    expert_down = scatter_about(key_list[8], (EXPERTS, FFE, D), FFE ** -0.5, 0.21875, ((0, 32),))
    routes_keys = jax.random.split(jax.random.fold_in(key_list[9], 1), TOKENS // TOK_LOC)
    routes_turns = jax.random.permutation(jax.random.fold_in(key_list[9], 3), TOKENS // TOK_LOC)
    routes = jax.vmap(lambda own, number: deal_out(jax.random.fold_in(key_list[9], 2), own, number, TOK_LOC, EXPERTS, TOP, CAP, 2))(routes_keys, routes_turns).reshape((TOKENS, TOP))
    route_weights = jnp.clip(jnp.exp(math.log(0.5) - 2.3025851 * jax.random.uniform(key_list[10], (TOKENS, TOP), jnp.float32) ** levels(key_list[10], (TOKENS, TOP), ((0, 32),), -0.2, 0.2)), 0.05, 0.5)
    return {"queries": queries, "keys": keys, "values": values, "distances": distances, "out_weight": out_weight, "residual": residual, "norm_gain": norm_gain, "expert_gate_up": expert_gate_up, "expert_down": expert_down, "routes": routes, "route_weights": route_weights}


def rounded(array):
    return lax.optimization_barrier(array.astype(jnp.bfloat16)).astype(jnp.float32)

def reference(queries, keys, values, distances, out_weight, residual, norm_gain, expert_gate_up, expert_down, routes, route_weights):
    groups = Q_HEADS // KV_HEADS
    shards = TOKENS // TOK_DEV
    blocks = TOK_DEV // BLK
    scale = 1.0 / math.sqrt(HD)
    query_all = queries.reshape(shards, TOK_DEV, KV_HEADS, groups, HD)
    key_all = keys.reshape(shards, TOK_DEV, KV_HEADS, HD)
    value_all = values.reshape(shards, TOK_DEV, KV_HEADS, HD)
    causal = jnp.arange(TOK_DEV)[:, None] >= jnp.arange(TOK_DEV)[None, :]
    head_index = jnp.arange(KV_HEADS, dtype=jnp.int32)[:, None]

    def one_shard(shard):
        query = query_all[shard].astype(jnp.float32)
        near_keys = key_all[shard].astype(jnp.float32)
        near_values = value_all[shard].astype(jnp.float32)
        local = jnp.einsum('tkgd,ukd->kgtu', query, near_keys) * scale
        local = jnp.where(causal, local, -jnp.inf)
        source = (shard - distances).astype(jnp.int32)
        usable = source >= 0
        clipped = jnp.maximum(source, 0).astype(jnp.int32)
        far_keys = key_all[clipped, :, head_index, :].astype(jnp.float32).reshape(KV_HEADS, DIST, blocks, BLK, HD)
        far_values = value_all[clipped, :, head_index, :].astype(jnp.float32).reshape(KV_HEADS, DIST, blocks, BLK, HD)
        query_blocks = query.reshape(blocks, BLK, KV_HEADS, groups, HD)
        remote = jnp.einsum('bqkgd,kjbud->kgjbqu', query_blocks, far_keys) * scale
        remote = jnp.where(usable[:, None, :, None, None, None], remote, -jnp.inf)
        highest = jnp.maximum(local.max(-1), remote.max(axis=(2, 5)).reshape(KV_HEADS, groups, TOK_DEV))
        near_weight = jnp.exp(local - highest[..., None])
        far_weight = jnp.exp(remote - highest.reshape(KV_HEADS, groups, blocks, BLK)[:, :, None, :, :, None])
        denominator = near_weight.sum(-1) + far_weight.sum(axis=(2, 5)).reshape(KV_HEADS, groups, TOK_DEV)
        mixed = jnp.einsum('kgtu,ukd->tkgd', rounded(near_weight), near_values)
        far_mixed = jnp.einsum('kgjbqu,kjbud->bqkgd', rounded(far_weight), far_values)
        mixed = mixed + far_mixed.reshape(TOK_DEV, KV_HEADS, groups, HD)
        mixed = mixed / jnp.transpose(denominator, (2, 0, 1))[..., None]
        return mixed.astype(jnp.bfloat16).reshape(TOK_DEV, Q_HEADS * HD)
    attention = lax.map(one_shard, jnp.arange(shards, dtype=jnp.int32)).reshape(TOKENS, Q_HEADS * HD)
    projected_all = jnp.dot(attention, out_weight, preferred_element_type=jnp.float32)
    attended = (residual.astype(jnp.float32) + projected_all).astype(jnp.bfloat16)
    widened = attended.astype(jnp.float32)
    inverse = lax.rsqrt(lax.optimization_barrier(jnp.mean(widened * widened, axis=-1, keepdims=True)) + 1e-06)
    normed = (widened * inverse * norm_gain).astype(jnp.bfloat16)
    entries = TOKENS * TOP
    limit = TOKENS // TOK_LOC * CAP
    flat_experts = routes.reshape(entries)
    flat_weights = route_weights.reshape(entries)
    owners = (jnp.arange(entries, dtype=jnp.int32) // TOP).astype(jnp.int32)

    def add_expert(expert, totals):
        expert = jnp.asarray(expert).astype(jnp.int32)
        chosen = flat_experts == expert
        places = jnp.cumsum(chosen.astype(jnp.int32), dtype=jnp.int32) - 1
        target = jnp.where(chosen, places, limit).astype(jnp.int32)
        picked = jnp.zeros((limit + 1,), jnp.int32).at[target].set(owners)[:limit]
        scales = jnp.zeros((limit + 1,), jnp.float32).at[target].set(flat_weights)[:limit]
        gate_up = lax.dynamic_index_in_dim(expert_gate_up, expert, 0, keepdims=False)
        down_matrix = lax.dynamic_index_in_dim(expert_down, expert, 0, keepdims=False)
        projected = jnp.dot(normed[picked], gate_up, preferred_element_type=jnp.float32)
        hidden = (jax.nn.silu(projected[:, :FFE]) * projected[:, FFE:]).astype(jnp.bfloat16)
        output = jnp.dot(hidden, down_matrix, preferred_element_type=jnp.float32)
        return totals.at[picked].add(scales[:, None] * rounded(output))
    totals = lax.fori_loop(0, EXPERTS, add_expert, jnp.zeros((TOKENS, D), jnp.float32))
    return (attended, totals.astype(jnp.bfloat16))
```

```python
import math

import jax
import jax.numpy as jnp
from jax import lax
from jax.sharding import PartitionSpec as P

HD = 128
FFE = 768
TOP = 8
EXP_DEV = 1
BLK = 128
DIST = 3


def expert_rows(arrived, expert_gate_up, expert_down, sources):
    width = arrived.shape[2]
    grid = arrived.reshape(sources, EXP_DEV, arrived.shape[1], width)
    projected = jnp.einsum(
        "sekd,edf->eskf", grid, expert_gate_up, preferred_element_type=jnp.float32
    )
    hidden = (jax.nn.silu(projected[..., :FFE]) * projected[..., FFE:]).astype(jnp.bfloat16)
    output = jnp.einsum("eskf,efd->sekd", hidden, expert_down, preferred_element_type=jnp.float32)
    return output.astype(jnp.bfloat16).reshape(arrived.shape)


def routed_experts(normed, expert_gate_up, expert_down, routes, route_weights, capacity):
    local_rows, width = normed.shape
    devices = lax.axis_size(("ctx", "head"))
    experts = devices * EXP_DEV
    flat_experts = routes.reshape(local_rows * TOP)
    onehot = (flat_experts[:, None] == jnp.arange(experts, dtype=jnp.int32)[None, :]).astype(
        jnp.int32
    )
    places = jnp.sum(jnp.cumsum(onehot, axis=0) * onehot, axis=1) - 1
    owners = jnp.arange(local_rows * TOP, dtype=jnp.int32) // TOP
    outgoing = (
        jnp.zeros((experts, capacity, width), jnp.bfloat16)
        .at[flat_experts, places]
        .set(normed[owners])
    )
    answered = expert_rows(
        lax.all_to_all(outgoing, ("ctx", "head"), split_axis=0, concat_axis=0, tiled=True),
        expert_gate_up,
        expert_down,
        devices,
    )
    returned = lax.all_to_all(answered, ("ctx", "head"), split_axis=0, concat_axis=0, tiled=True)
    picked = returned[flat_experts, places].astype(jnp.float32)
    weighted = route_weights.reshape(local_rows * TOP)[:, None] * picked
    moe_out = weighted.reshape(local_rows, TOP, width).sum(axis=1).astype(jnp.bfloat16)
    return moe_out


def dense_experts(normed, expert_gate_up, expert_down, table, capacity):
    local_rows, width = normed.shape
    axes = ("ctx", "head")
    sources = table.shape[0]
    mine = lax.axis_index(axes).astype(jnp.float32)
    chosen = table[:, :, :TOP] == mine
    weight = jnp.sum(jnp.where(chosen, table[:, :, TOP:], 0.0), axis=2)
    named = jnp.any(chosen, axis=2)
    earlier = jnp.arange(local_rows)[:, None] < jnp.arange(local_rows)[None, :]
    places = jnp.dot(
        named.astype(jnp.bfloat16), earlier.astype(jnp.bfloat16), preferred_element_type=jnp.float32
    ).astype(jnp.int32)
    select = (
        named[:, None, :] & (places[:, None, :] == jnp.arange(capacity, dtype=jnp.int32)[None, :, None])
    ).astype(jnp.bfloat16)
    everyone = lax.all_gather(normed, axes, axis=0, tiled=False)
    rows = jnp.einsum(
        "sct,std->scd", select, everyone, preferred_element_type=jnp.float32
    ).astype(jnp.bfloat16)
    rows = rows.reshape(sources * capacity, width)
    projected = jnp.dot(rows, expert_gate_up[0], preferred_element_type=jnp.float32)
    hidden = (jax.nn.silu(projected[:, :FFE]) * projected[:, FFE:]).astype(jnp.bfloat16)
    output = jnp.dot(hidden, expert_down[0], preferred_element_type=jnp.float32).astype(jnp.bfloat16)
    output = output.reshape(sources, capacity, width)
    spread = jnp.einsum("sct,scd->std", select, output, preferred_element_type=jnp.float32)
    partial = (weight[:, :, None] * spread).astype(jnp.bfloat16)
    return lax.psum_scatter(
        partial.reshape(sources * local_rows, width), axes, scatter_dimension=0, tiled=True
    )


def body(
    queries,
    keys,
    values,
    distances,
    out_weight,
    residual,
    norm_gain,
    expert_gate_up,
    expert_down,
    routes,
    route_weights,
):
    length = queries.shape[0]
    groups = queries.shape[1] // HD
    blocks = length // BLK
    scale = 1.0 / math.sqrt(HD)
    table = lax.all_gather(
        jnp.concatenate([routes.astype(jnp.float32), route_weights], axis=1),
        ("ctx", "head"),
        axis=0,
        tiled=False,
    )
    wanted = distances[0]
    source = lax.axis_index("ctx") - wanted
    usable = source >= 0
    packed = jnp.concatenate([keys, values], axis=1)
    everything = lax.all_gather(packed, "ctx", axis=0, tiled=True)
    offsets = jnp.maximum(source, 0) * length
    fetched = jnp.stack(
        [
            lax.dynamic_slice_in_dim(everything, offsets[slot_index], length, 0)
            for slot_index in range(DIST)
        ]
    )
    query = queries.reshape(length, groups, HD)
    causal = jnp.arange(length)[:, None] >= jnp.arange(length)[None, :]
    local = jnp.einsum("tgd,ud->gtu", query, keys, preferred_element_type=jnp.float32) * scale
    local = jnp.where(causal[None], local, -jnp.inf)
    far_keys = fetched[:, :, :HD].reshape(DIST, blocks, BLK, HD)
    far_values = fetched[:, :, HD:].reshape(DIST, blocks, BLK, HD)
    query_blocks = queries.reshape(blocks, BLK, groups, HD)
    remote = (
        jnp.einsum("bqgd,jbud->gjbqu", query_blocks, far_keys, preferred_element_type=jnp.float32)
        * scale
    )
    remote = jnp.where(usable[None, :, None, None, None], remote, -jnp.inf)
    highest = jnp.maximum(local.max(-1), remote.max(axis=(1, 4)).reshape(groups, length))
    near_weight = jnp.exp(local - highest[:, :, None])
    far_weight = jnp.exp(remote - highest.reshape(groups, blocks, BLK)[:, None, :, :, None])
    denominator = near_weight.sum(-1) + far_weight.sum(axis=(1, 4)).reshape(groups, length)
    mixed = jnp.einsum(
        "gtu,ud->tgd", near_weight.astype(jnp.bfloat16), values, preferred_element_type=jnp.float32
    )
    far_mixed = jnp.einsum(
        "gjbqu,jbud->bqgd",
        far_weight.astype(jnp.bfloat16),
        far_values,
        preferred_element_type=jnp.float32,
    )
    mixed = mixed + far_mixed.reshape(length, groups, HD)
    attention = (
        (mixed / jnp.transpose(denominator)[:, :, None])
        .astype(jnp.bfloat16)
        .reshape(length, groups * HD)
    )
    summed = lax.psum_scatter(
        jnp.dot(attention, out_weight, preferred_element_type=jnp.float32).astype(jnp.bfloat16),
        "head",
        scatter_dimension=0,
        tiled=True,
    )
    attended = (residual.astype(jnp.float32) + summed.astype(jnp.float32)).astype(jnp.bfloat16)
    widened = attended.astype(jnp.float32)
    inverse = lax.rsqrt(jnp.mean(widened * widened, axis=-1, keepdims=True) + 1e-06)
    normed = (widened * inverse * norm_gain).astype(jnp.bfloat16)
    local_rows = normed.shape[0]
    width = normed.shape[1]
    devices = lax.axis_size(("ctx", "head"))
    experts = devices * EXP_DEV
    capacity = max(2, 2 * local_rows * TOP // experts)
    if devices * local_rows <= 2 * experts * capacity:
        moe_out = dense_experts(
            normed, expert_gate_up, expert_down, table, capacity
        )
    else:
        moe_out = routed_experts(
            normed, expert_gate_up, expert_down, routes, route_weights, capacity
        )
    return (attended, moe_out)


def solution(mesh):
    return jax.shard_map(
        body,
        mesh=mesh,
        in_specs=(
            P("ctx", "head"),
            P("ctx", "head"),
            P("ctx", "head"),
            P("head", None),
            P("head", None),
            P(("ctx", "head"), None),
            P(),
            P(("ctx", "head"), None, None),
            P(("ctx", "head"), None, None),
            P(("ctx", "head"), None),
            P(("ctx", "head"), None),
        ),
        out_specs=(P(("ctx", "head"), None), P(("ctx", "head"), None)),
        check_vma=False,
    )
```

```python
import math

import jax
import jax.numpy as jnp
from jax import lax
from jax.sharding import PartitionSpec as P

HD = 128
FFE = 768
TOP = 8
EXP_DEV = 1
BLK = 128
DIST = 3
CHUNKS = 2


def expert_rows(arrived, expert_gate_up, expert_down, sources):
    width = arrived.shape[2]
    grid = arrived.reshape(sources, EXP_DEV, arrived.shape[1], width)
    projected = jnp.einsum(
        "sekd,edf->eskf", grid, expert_gate_up, preferred_element_type=jnp.float32
    )
    hidden = (jax.nn.silu(projected[..., :FFE]) * projected[..., FFE:]).astype(jnp.bfloat16)
    output = jnp.einsum("eskf,efd->sekd", hidden, expert_down, preferred_element_type=jnp.float32)
    return output.astype(jnp.bfloat16).reshape(arrived.shape)


def bits_of(axis):
    return [(axis, 1 << at) for at in range(lax.axis_size(axis).bit_length() - 1)]


def halve(total, axis, bit, dim):
    size = lax.axis_size(axis)
    mine = (lax.axis_index(axis) // bit) % 2
    sent = lax.dynamic_index_in_dim(total, 1 - mine, dim, keepdims=False)
    kept = lax.dynamic_index_in_dim(total, mine, dim, keepdims=False)
    got = lax.ppermute(sent, axis, [(i, i ^ bit) for i in range(size)])
    return (kept.astype(jnp.float32) + got.astype(jnp.float32)).astype(jnp.bfloat16)


def halve_all(total, names, order):
    names = list(names)
    for axis, bit in order:
        dim = names.index((axis, bit))
        total = halve(total, axis, bit, dim)
        names.pop(dim)
    return total


def routed_experts(normed, expert_gate_up, expert_down, routes, route_weights, capacity):
    local_rows, width = normed.shape
    devices = lax.axis_size(("ctx", "head"))
    experts = devices * EXP_DEV
    flat_experts = routes.reshape(local_rows * TOP)
    onehot = (flat_experts[:, None] == jnp.arange(experts, dtype=jnp.int32)[None, :]).astype(
        jnp.int32
    )
    places = jnp.sum(jnp.cumsum(onehot, axis=0) * onehot, axis=1) - 1
    owners = jnp.arange(local_rows * TOP, dtype=jnp.int32) // TOP
    outgoing = (
        jnp.zeros((experts, capacity, width), jnp.bfloat16)
        .at[flat_experts, places]
        .set(normed[owners])
    )
    answered = expert_rows(
        lax.all_to_all(outgoing, ("ctx", "head"), split_axis=0, concat_axis=0, tiled=True),
        expert_gate_up,
        expert_down,
        devices,
    )
    returned = lax.all_to_all(answered, ("ctx", "head"), split_axis=0, concat_axis=0, tiled=True)
    picked = returned[flat_experts, places].astype(jnp.float32)
    weighted = route_weights.reshape(local_rows * TOP)[:, None] * picked
    moe_out = weighted.reshape(local_rows, TOP, width).sum(axis=1).astype(jnp.bfloat16)
    return moe_out


def dense_experts(normed, expert_gate_up, expert_down, table, capacity):
    local_rows, width = normed.shape
    axes = ("ctx", "head")
    sources = table.shape[0]
    mine = lax.axis_index(axes).astype(jnp.float32)
    chosen = table[:, :, :TOP] == mine
    weight = jnp.sum(jnp.where(chosen, table[:, :, TOP:], 0.0), axis=2)
    named = jnp.any(chosen, axis=2)
    earlier = jnp.arange(local_rows)[:, None] < jnp.arange(local_rows)[None, :]
    places = jnp.dot(
        named.astype(jnp.bfloat16), earlier.astype(jnp.bfloat16), preferred_element_type=jnp.float32
    ).astype(jnp.int32)
    select = (
        named[:, None, :] & (places[:, None, :] == jnp.arange(capacity, dtype=jnp.int32)[None, :, None])
    ).astype(jnp.bfloat16)
    everyone = lax.all_gather(normed, axes, axis=0, tiled=False)
    rows = jnp.einsum(
        "sct,std->scd", select, everyone, preferred_element_type=jnp.float32
    ).astype(jnp.bfloat16)
    rows = rows.reshape(sources * capacity, width)
    projected = jnp.dot(rows, expert_gate_up[0], preferred_element_type=jnp.float32)
    hidden = (jax.nn.silu(projected[:, :FFE]) * projected[:, FFE:]).astype(jnp.bfloat16)
    near, far = bits_of("head"), bits_of("ctx")
    names = far[::-1] + near[::-1]
    orders = (
        near[:1] + far[:1] + near[1:] + far[1:],
        near + far,
    )
    chunk = width // CHUNKS
    core_dim = names.index(near[0])
    core = lax.axis_index("head") % 2
    shape = [2] * len(names)
    weight = weight.reshape(shape + [local_rows])
    select = select.reshape(shape + [capacity, local_rows])
    results = []
    for number in range(CHUNKS):
        columns = slice(number * chunk, (number + 1) * chunk)
        output = jnp.dot(
            hidden, expert_down[0, :, columns], preferred_element_type=jnp.float32
        ).astype(jnp.bfloat16)
        output = output.reshape(shape + [capacity, chunk])

        def side(which):
            chosen_rows = lax.dynamic_index_in_dim(select, which, core_dim, keepdims=False)
            held = lax.dynamic_index_in_dim(output, which, core_dim, keepdims=False)
            scale = lax.dynamic_index_in_dim(weight, which, core_dim, keepdims=False)
            flat = sources // 2
            spread = jnp.einsum(
                "sct,scd->std",
                chosen_rows.reshape(flat, capacity, local_rows),
                held.reshape(flat, capacity, chunk),
                preferred_element_type=jnp.float32,
            )
            return (scale.reshape(flat, local_rows, 1) * spread).astype(jnp.bfloat16)

        swap = [(i, i ^ 1) for i in range(lax.axis_size("head"))]
        got = lax.ppermute(side(1 - core), "head", swap)
        total = (side(core).astype(jnp.float32) + got.astype(jnp.float32)).astype(jnp.bfloat16)
        total = total.reshape(shape[1:] + [local_rows, chunk])
        left = [name for name in names if name != near[0]]
        results.append(halve_all(total, left, orders[number % 2][1:]))
    return jnp.concatenate(results, axis=1)


def body(
    queries,
    keys,
    values,
    distances,
    out_weight,
    residual,
    norm_gain,
    expert_gate_up,
    expert_down,
    routes,
    route_weights,
):
    length = queries.shape[0]
    groups = queries.shape[1] // HD
    blocks = length // BLK
    scale = 1.0 / math.sqrt(HD)
    table = lax.all_gather(
        jnp.concatenate([routes.astype(jnp.float32), route_weights], axis=1),
        ("ctx", "head"),
        axis=0,
        tiled=False,
    )
    wanted = distances[0]
    source = lax.axis_index("ctx") - wanted
    usable = source >= 0
    packed = jnp.concatenate([keys, values], axis=1)
    everything = lax.all_gather(packed, "ctx", axis=0, tiled=True)
    offsets = jnp.maximum(source, 0) * length
    fetched = jnp.stack(
        [
            lax.dynamic_slice_in_dim(everything, offsets[slot_index], length, 0)
            for slot_index in range(DIST)
        ]
    )
    query = queries.reshape(length, groups, HD)
    causal = jnp.arange(length)[:, None] >= jnp.arange(length)[None, :]
    local = jnp.einsum("tgd,ud->gtu", query, keys, preferred_element_type=jnp.float32) * scale
    local = jnp.where(causal[None], local, -jnp.inf)
    far_keys = fetched[:, :, :HD].reshape(DIST, blocks, BLK, HD)
    far_values = fetched[:, :, HD:].reshape(DIST, blocks, BLK, HD)
    query_blocks = queries.reshape(blocks, BLK, groups, HD)
    remote = (
        jnp.einsum("bqgd,jbud->gjbqu", query_blocks, far_keys, preferred_element_type=jnp.float32)
        * scale
    )
    remote = jnp.where(usable[None, :, None, None, None], remote, -jnp.inf)
    highest = jnp.maximum(local.max(-1), remote.max(axis=(1, 4)).reshape(groups, length))
    near_weight = jnp.exp(local - highest[:, :, None])
    far_weight = jnp.exp(remote - highest.reshape(groups, blocks, BLK)[:, None, :, :, None])
    denominator = near_weight.sum(-1) + far_weight.sum(axis=(1, 4)).reshape(groups, length)
    mixed = jnp.einsum(
        "gtu,ud->tgd", near_weight.astype(jnp.bfloat16), values, preferred_element_type=jnp.float32
    )
    far_mixed = jnp.einsum(
        "gjbqu,jbud->bqgd",
        far_weight.astype(jnp.bfloat16),
        far_values,
        preferred_element_type=jnp.float32,
    )
    mixed = mixed + far_mixed.reshape(length, groups, HD)
    attention = (
        (mixed / jnp.transpose(denominator)[:, :, None])
        .astype(jnp.bfloat16)
        .reshape(length, groups * HD)
    )
    projected = jnp.dot(attention, out_weight, preferred_element_type=jnp.float32).astype(
        jnp.bfloat16
    )
    near = bits_of("head")
    pieces = projected.reshape([2] * len(near) + [residual.shape[0], residual.shape[1]])
    summed = halve_all(pieces, near[::-1], near)
    attended = (residual.astype(jnp.float32) + summed.astype(jnp.float32)).astype(jnp.bfloat16)
    widened = attended.astype(jnp.float32)
    inverse = lax.rsqrt(jnp.mean(widened * widened, axis=-1, keepdims=True) + 1e-06)
    normed = (widened * inverse * norm_gain).astype(jnp.bfloat16)
    local_rows = normed.shape[0]
    width = normed.shape[1]
    devices = lax.axis_size(("ctx", "head"))
    experts = devices * EXP_DEV
    capacity = max(2, 2 * local_rows * TOP // experts)
    if devices * local_rows <= 2 * experts * capacity:
        moe_out = dense_experts(
            normed, expert_gate_up, expert_down, table, capacity
        )
    else:
        moe_out = routed_experts(
            normed, expert_gate_up, expert_down, routes, route_weights, capacity
        )
    return (attended, moe_out)


def solution(mesh):
    return jax.shard_map(
        body,
        mesh=mesh,
        in_specs=(
            P("ctx", "head"),
            P("ctx", "head"),
            P("ctx", "head"),
            P("head", None),
            P("head", None),
            P(("ctx", "head"), None),
            P(),
            P(("ctx", "head"), None, None),
            P(("ctx", "head"), None, None),
            P(("ctx", "head"), None),
            P(("ctx", "head"), None),
        ),
        out_specs=(P(("ctx", "head"), None), P(("ctx", "head"), None)),
        check_vma=False,
    )
```

```python
import math

import jax
import jax.numpy as jnp
from jax import lax
from jax.sharding import PartitionSpec as P

HD = 128
FFE = 768
TOP = 8
EXP_DEV = 1
BLK = 128
DIST = 3
CHUNKS = 4


def expert_rows(arrived, expert_gate_up, expert_down, sources):
    width = arrived.shape[2]
    grid = arrived.reshape(sources, EXP_DEV, arrived.shape[1], width)
    projected = jnp.einsum(
        "sekd,edf->eskf", grid, expert_gate_up, preferred_element_type=jnp.float32
    )
    hidden = (jax.nn.silu(projected[..., :FFE]) * projected[..., FFE:]).astype(jnp.bfloat16)
    output = jnp.einsum("eskf,efd->sekd", hidden, expert_down, preferred_element_type=jnp.float32)
    return output.astype(jnp.bfloat16).reshape(arrived.shape)


def bits_of(axis):
    return [(axis, 1 << at) for at in range(lax.axis_size(axis).bit_length() - 1)]


def swapped(array, axis, bit):
    return lax.ppermute(array, axis, [(i, i ^ bit) for i in range(lax.axis_size(axis))])


def double_all(array, order):
    for axis, bit in order:
        array = jnp.stack([array, swapped(array, axis, bit)])
    return array


def add(kept, got):
    return (kept.astype(jnp.float32) + got.astype(jnp.float32)).astype(jnp.bfloat16)


def halve_all(total, names, order):
    names = list(names)
    for axis, bit in order:
        dim = names.index((axis, bit))
        sent = lax.index_in_dim(total, 1, dim, keepdims=False)
        kept = lax.index_in_dim(total, 0, dim, keepdims=False)
        total = add(kept, swapped(sent, axis, bit))
        names.pop(dim)
    return total


def routed_experts(normed, expert_gate_up, expert_down, routes, route_weights, capacity):
    local_rows, width = normed.shape
    devices = lax.axis_size(("ctx", "head"))
    experts = devices * EXP_DEV
    flat_experts = routes.reshape(local_rows * TOP)
    onehot = (flat_experts[:, None] == jnp.arange(experts, dtype=jnp.int32)[None, :]).astype(
        jnp.int32
    )
    places = jnp.sum(jnp.cumsum(onehot, axis=0) * onehot, axis=1) - 1
    owners = jnp.arange(local_rows * TOP, dtype=jnp.int32) // TOP
    outgoing = (
        jnp.zeros((experts, capacity, width), jnp.bfloat16)
        .at[flat_experts, places]
        .set(normed[owners])
    )
    answered = expert_rows(
        lax.all_to_all(outgoing, ("ctx", "head"), split_axis=0, concat_axis=0, tiled=True),
        expert_gate_up,
        expert_down,
        devices,
    )
    returned = lax.all_to_all(answered, ("ctx", "head"), split_axis=0, concat_axis=0, tiled=True)
    picked = returned[flat_experts, places].astype(jnp.float32)
    weighted = route_weights.reshape(local_rows * TOP)[:, None] * picked
    moe_out = weighted.reshape(local_rows, TOP, width).sum(axis=1).astype(jnp.bfloat16)
    return moe_out


def dense_experts(normed, expert_gate_up, expert_down, routes, route_weights, capacity):
    local_rows, width = normed.shape
    near, far = bits_of("head"), bits_of("ctx")
    names = far[::-1] + near[::-1]
    core = names[-1]
    rest = names[:-1]
    orders = (far[:1] + near[1:] + far[1:], near[1:] + far)
    shape = [2] * len(rest)
    half = 2 ** len(rest)
    table = double_all(
        jnp.concatenate([routes.astype(jnp.float32), route_weights], axis=1),
        rest[::-1] + [core],
    ).reshape(2 * half, local_rows, 2 * TOP)
    mine = lax.axis_index(("ctx", "head")).astype(jnp.float32)
    chosen = table[:, :, :TOP] == mine
    weight = jnp.sum(jnp.where(chosen, table[:, :, TOP:], 0.0), axis=2)
    named = jnp.any(chosen, axis=2)
    earlier = jnp.arange(local_rows)[:, None] < jnp.arange(local_rows)[None, :]
    places = jnp.dot(
        named.astype(jnp.bfloat16), earlier.astype(jnp.bfloat16), preferred_element_type=jnp.float32
    ).astype(jnp.int32)
    select = (
        named[:, None, :] & (places[:, None, :] == jnp.arange(capacity, dtype=jnp.int32)[None, :, None])
    ).astype(jnp.bfloat16)
    select = select.reshape(2, half, capacity, local_rows)
    weight = weight.reshape(2, half, local_rows)
    chunk = width // CHUNKS
    picked = ([], [])
    for number in range(CHUNKS):
        order = orders[number % 2][::-1]
        held = double_all(normed[:, number * chunk : (number + 1) * chunk], order)
        for side, blocks in enumerate((held, swapped(held, *core))):
            blocks = jnp.transpose(
                blocks, [order[::-1].index(name) for name in rest] + [len(rest), len(rest) + 1]
            ).reshape(half, local_rows, chunk)
            picked[side].append(
                jnp.einsum(
                    "sct,std->scd", select[side], blocks, preferred_element_type=jnp.float32
                ).astype(jnp.bfloat16)
            )
    hidden = []
    for side in range(2):
        rows = jnp.concatenate(picked[side], axis=2).reshape(half * capacity, width)
        projected = jnp.dot(rows, expert_gate_up[0], preferred_element_type=jnp.float32)
        hidden.append((jax.nn.silu(projected[:, :FFE]) * projected[:, FFE:]).astype(jnp.bfloat16))
    results = []
    for number in range(CHUNKS):
        columns = slice(number * chunk, (number + 1) * chunk)
        partial = []
        for side in range(2):
            output = jnp.dot(
                hidden[side], expert_down[0, :, columns], preferred_element_type=jnp.float32
            ).astype(jnp.bfloat16)
            spread = jnp.einsum(
                "sct,scd->std",
                select[side],
                output.reshape(half, capacity, chunk),
                preferred_element_type=jnp.float32,
            )
            partial.append((weight[side][:, :, None] * spread).astype(jnp.bfloat16))
        total = add(partial[0], swapped(partial[1], *core)).reshape(shape + [local_rows, chunk])
        results.append(halve_all(total, rest, orders[number % 2]))
    return jnp.concatenate(results, axis=1)


def body(
    queries,
    keys,
    values,
    distances,
    out_weight,
    residual,
    norm_gain,
    expert_gate_up,
    expert_down,
    routes,
    route_weights,
):
    length = queries.shape[0]
    groups = queries.shape[1] // HD
    blocks = length // BLK
    scale = 1.0 / math.sqrt(HD)
    wanted = distances[0]
    source = lax.axis_index("ctx") - wanted
    usable = source >= 0
    far = bits_of("ctx")
    every_key = double_all(keys, far[::-1]).reshape(-1, HD)
    every_value = double_all(values, far[:1] + far[:0:-1]).reshape(-1, HD)
    apart = jnp.maximum(source, 0) ^ lax.axis_index("ctx")
    shards = lax.axis_size("ctx")
    turned = sum(
        ((apart // bit) % 2) * (shards // 2 // bit) for axis, bit in far
    )
    key_offsets = turned * length
    value_bits = far[1:][::1] + far[:1]
    value_offsets = length * sum(
        ((apart // bit) % 2) * (shards >> (place + 1)) for place, (axis, bit) in enumerate(value_bits)
    )
    fetched_keys = jnp.stack(
        [
            lax.dynamic_slice_in_dim(every_key, key_offsets[slot_index], length, 0)
            for slot_index in range(DIST)
        ]
    )
    fetched_values = jnp.stack(
        [
            lax.dynamic_slice_in_dim(every_value, value_offsets[slot_index], length, 0)
            for slot_index in range(DIST)
        ]
    )
    query = queries.reshape(length, groups, HD)
    causal = jnp.arange(length)[:, None] >= jnp.arange(length)[None, :]
    local = jnp.einsum("tgd,ud->gtu", query, keys, preferred_element_type=jnp.float32) * scale
    local = jnp.where(causal[None], local, -jnp.inf)
    far_keys = fetched_keys.reshape(DIST, blocks, BLK, HD)
    far_values = fetched_values.reshape(DIST, blocks, BLK, HD)
    query_blocks = queries.reshape(blocks, BLK, groups, HD)
    remote = (
        jnp.einsum("bqgd,jbud->gjbqu", query_blocks, far_keys, preferred_element_type=jnp.float32)
        * scale
    )
    remote = jnp.where(usable[None, :, None, None, None], remote, -jnp.inf)
    highest = jnp.maximum(local.max(-1), remote.max(axis=(1, 4)).reshape(groups, length))
    near_weight = jnp.exp(local - highest[:, :, None])
    far_weight = jnp.exp(remote - highest.reshape(groups, blocks, BLK)[:, None, :, :, None])
    denominator = near_weight.sum(-1) + far_weight.sum(axis=(1, 4)).reshape(groups, length)
    mixed = jnp.einsum(
        "gtu,ud->tgd", near_weight.astype(jnp.bfloat16), values, preferred_element_type=jnp.float32
    )
    far_mixed = jnp.einsum(
        "gjbqu,jbud->bqgd",
        far_weight.astype(jnp.bfloat16),
        far_values,
        preferred_element_type=jnp.float32,
    )
    mixed = mixed + far_mixed.reshape(length, groups, HD)
    attention = (
        (mixed / jnp.transpose(denominator)[:, :, None])
        .astype(jnp.bfloat16)
        .reshape(length, groups * HD)
    )
    near = bits_of("head")
    heads = lax.axis_size("head")
    turned_rows = jnp.concatenate(
        [
            lax.dynamic_slice_in_dim(
                attention, (lax.axis_index("head") ^ block) * residual.shape[0], residual.shape[0], 0
            )
            for block in range(heads)
        ]
    )
    pieces = jnp.dot(turned_rows, out_weight, preferred_element_type=jnp.float32).astype(
        jnp.bfloat16
    )
    pieces = pieces.reshape([2] * len(near) + list(residual.shape))
    summed = halve_all(pieces, near[::-1], near)
    attended = (residual.astype(jnp.float32) + summed.astype(jnp.float32)).astype(jnp.bfloat16)
    widened = attended.astype(jnp.float32)
    inverse = lax.rsqrt(jnp.mean(widened * widened, axis=-1, keepdims=True) + 1e-06)
    normed = (widened * inverse * norm_gain).astype(jnp.bfloat16)
    local_rows = normed.shape[0]
    width = normed.shape[1]
    devices = lax.axis_size(("ctx", "head"))
    experts = devices * EXP_DEV
    capacity = max(2, 2 * local_rows * TOP // experts)
    if devices * local_rows <= 2 * experts * capacity:
        moe_out = dense_experts(
            normed, expert_gate_up, expert_down, routes, route_weights, capacity
        )
    else:
        moe_out = routed_experts(
            normed, expert_gate_up, expert_down, routes, route_weights, capacity
        )
    return (attended, moe_out)


def solution(mesh):
    return jax.shard_map(
        body,
        mesh=mesh,
        in_specs=(
            P("ctx", "head"),
            P("ctx", "head"),
            P("ctx", "head"),
            P("head", None),
            P("head", None),
            P(("ctx", "head"), None),
            P(),
            P(("ctx", "head"), None, None),
            P(("ctx", "head"), None, None),
            P(("ctx", "head"), None),
            P(("ctx", "head"), None),
        ),
        out_specs=(P(("ctx", "head"), None), P(("ctx", "head"), None)),
        check_vma=False,
    )
```

```python
import math

import jax
import jax.numpy as jnp
from jax import lax
from jax.sharding import PartitionSpec as P

HD = 128
FFE = 768
TOP = 8
EXP_DEV = 1
BLK = 128
DIST = 3


def expert_rows(arrived, expert_gate_up, expert_down, sources):
    width = arrived.shape[2]
    grid = arrived.reshape(sources, EXP_DEV, arrived.shape[1], width)
    projected = jnp.einsum(
        "sekd,edf->eskf", grid, expert_gate_up, preferred_element_type=jnp.float32
    )
    hidden = (jax.nn.silu(projected[..., :FFE]) * projected[..., FFE:]).astype(jnp.bfloat16)
    output = jnp.einsum("eskf,efd->sekd", hidden, expert_down, preferred_element_type=jnp.float32)
    return output.astype(jnp.bfloat16).reshape(arrived.shape)


def bits_of(axis):
    return [(axis, 1 << at) for at in range(lax.axis_size(axis).bit_length() - 1)]


def swapped(array, axis, bit):
    return lax.ppermute(array, axis, [(i, i ^ bit) for i in range(lax.axis_size(axis))])


def double_all(array, order):
    for axis, bit in order:
        array = jnp.stack([array, swapped(array, axis, bit)])
    return array


def add(kept, got):
    return (kept.astype(jnp.float32) + got.astype(jnp.float32)).astype(jnp.bfloat16)


def halve_all(total, names, order):
    names = list(names)
    for axis, bit in order:
        dim = names.index((axis, bit))
        sent = lax.index_in_dim(total, 1, dim, keepdims=False)
        kept = lax.index_in_dim(total, 0, dim, keepdims=False)
        total = add(kept, swapped(sent, axis, bit))
        names.pop(dim)
    return total


def routed_experts(normed, expert_gate_up, expert_down, routes, route_weights, capacity):
    local_rows, width = normed.shape
    devices = lax.axis_size(("ctx", "head"))
    experts = devices * EXP_DEV
    flat_experts = routes.reshape(local_rows * TOP)
    onehot = (flat_experts[:, None] == jnp.arange(experts, dtype=jnp.int32)[None, :]).astype(
        jnp.int32
    )
    places = jnp.sum(jnp.cumsum(onehot, axis=0) * onehot, axis=1) - 1
    owners = jnp.arange(local_rows * TOP, dtype=jnp.int32) // TOP
    outgoing = (
        jnp.zeros((experts, capacity, width), jnp.bfloat16)
        .at[flat_experts, places]
        .set(normed[owners])
    )
    answered = expert_rows(
        lax.all_to_all(outgoing, ("ctx", "head"), split_axis=0, concat_axis=0, tiled=True),
        expert_gate_up,
        expert_down,
        devices,
    )
    returned = lax.all_to_all(answered, ("ctx", "head"), split_axis=0, concat_axis=0, tiled=True)
    picked = returned[flat_experts, places].astype(jnp.float32)
    weighted = route_weights.reshape(local_rows * TOP)[:, None] * picked
    moe_out = weighted.reshape(local_rows, TOP, width).sum(axis=1).astype(jnp.bfloat16)
    return moe_out


def dense_experts(normed, expert_gate_up, expert_down, routes, route_weights, capacity):
    local_rows, width = normed.shape
    near, far = bits_of("head"), bits_of("ctx")
    names = far[::-1] + near[::-1]
    core = names[-1]
    rest = names[:-1]
    straight, crossed = far[:1] + near[1:] + far[1:], near[1:] + far
    orders = (straight, crossed, far[1:] + far[:1] + near[1:], straight, crossed)
    delays = (0, 0, 0, 1, 1)
    widths = [share * width // 16 for share in (4, 4, 4, 2, 2)]
    starts = [sum(widths[:number]) for number in range(len(widths))]
    chunks = range(len(widths))
    steps = len(rest) + max(delays)
    shape = [2] * len(rest)
    half = 2 ** len(rest)
    table = double_all(
        jnp.concatenate([routes.astype(jnp.float32), route_weights], axis=1),
        rest[::-1] + [core],
    ).reshape(2 * half, local_rows, 2 * TOP)
    mine = lax.axis_index(("ctx", "head")).astype(jnp.float32)
    chosen = table[:, :, :TOP] == mine
    weight = jnp.sum(jnp.where(chosen, table[:, :, TOP:], 0.0), axis=2)
    named = jnp.any(chosen, axis=2)
    earlier = jnp.arange(local_rows)[:, None] < jnp.arange(local_rows)[None, :]
    places = jnp.dot(
        named.astype(jnp.bfloat16), earlier.astype(jnp.bfloat16), preferred_element_type=jnp.float32
    ).astype(jnp.int32)
    select = (
        named[:, None, :] & (places[:, None, :] == jnp.arange(capacity, dtype=jnp.int32)[None, :, None])
    ).astype(jnp.bfloat16)
    select = select.reshape(2, half, capacity, local_rows)
    weight = weight.reshape(2, half, local_rows)
    held = [normed[:, starts[n] : starts[n] + widths[n]] for n in chunks]
    for step in range(steps)[::-1]:
        active = [n for n in chunks if 0 <= step - delays[n] < len(rest)]
        if step < steps - 1:
            for n, array in zip(active, lax.optimization_barrier([held[n] for n in active])):
                held[n] = array
        for n in active:
            held[n] = double_all(held[n], [orders[n][step - delays[n]]])
    projected = [0.0, 0.0]
    for n in sorted(chunks, key=lambda n: -delays[n]):
        for side, blocks in enumerate((held[n], swapped(held[n], *core))):
            blocks = jnp.transpose(
                blocks, [orders[n].index(name) for name in rest] + [len(rest), len(rest) + 1]
            ).reshape(half, local_rows, widths[n])
            rows = jnp.einsum(
                "sct,std->scd", select[side], blocks, preferred_element_type=jnp.float32
            ).astype(jnp.bfloat16)
            projected[side] = projected[side] + jnp.dot(
                rows.reshape(half * capacity, widths[n]),
                expert_gate_up[0, starts[n] : starts[n] + widths[n]],
                preferred_element_type=jnp.float32,
            )
    hidden = [
        (jax.nn.silu(both[:, :FFE]) * both[:, FFE:]).astype(jnp.bfloat16) for both in projected
    ]
    totals = []
    for n in chunks:
        columns = slice(starts[n], starts[n] + widths[n])
        partial = []
        for side in range(2):
            output = jnp.dot(
                hidden[side], expert_down[0, :, columns], preferred_element_type=jnp.float32
            ).astype(jnp.bfloat16)
            spread = jnp.einsum(
                "sct,scd->std",
                select[side],
                output.reshape(half, capacity, widths[n]),
                preferred_element_type=jnp.float32,
            )
            partial.append((weight[side][:, :, None] * spread).astype(jnp.bfloat16))
        total = add(partial[0], swapped(partial[1], *core))
        totals.append(total.reshape(shape + [local_rows, widths[n]]))
    left = [list(rest) for n in chunks]
    for step in range(steps):
        active = [n for n in chunks if 0 <= step - delays[n] < len(rest)]
        if step:
            for n, array in zip(active, lax.optimization_barrier([totals[n] for n in active])):
                totals[n] = array
        for n in active:
            name = orders[n][step - delays[n]]
            totals[n] = halve_all(totals[n], left[n], [name])
            left[n].remove(name)
    return jnp.concatenate(totals, axis=1)


def body(
    queries,
    keys,
    values,
    distances,
    out_weight,
    residual,
    norm_gain,
    expert_gate_up,
    expert_down,
    routes,
    route_weights,
):
    length = queries.shape[0]
    groups = queries.shape[1] // HD
    blocks = length // BLK
    scale = 1.0 / math.sqrt(HD)
    wanted = distances[0]
    source = lax.axis_index("ctx") - wanted
    usable = source >= 0
    far = bits_of("ctx")
    every_key = double_all(keys, far[::-1]).reshape(-1, HD)
    every_value = double_all(values, far[:1] + far[:0:-1]).reshape(-1, HD)
    apart = jnp.maximum(source, 0) ^ lax.axis_index("ctx")
    shards = lax.axis_size("ctx")
    turned = sum(
        ((apart // bit) % 2) * (shards // 2 // bit) for axis, bit in far
    )
    key_offsets = turned * length
    value_bits = far[1:][::1] + far[:1]
    value_offsets = length * sum(
        ((apart // bit) % 2) * (shards >> (place + 1)) for place, (axis, bit) in enumerate(value_bits)
    )
    fetched_keys = jnp.stack(
        [
            lax.dynamic_slice_in_dim(every_key, key_offsets[slot_index], length, 0)
            for slot_index in range(DIST)
        ]
    )
    fetched_values = jnp.stack(
        [
            lax.dynamic_slice_in_dim(every_value, value_offsets[slot_index], length, 0)
            for slot_index in range(DIST)
        ]
    )
    query = queries.reshape(length, groups, HD)
    causal = jnp.arange(length)[:, None] >= jnp.arange(length)[None, :]
    local = jnp.einsum("tgd,ud->gtu", query, keys, preferred_element_type=jnp.float32) * scale
    local = jnp.where(causal[None], local, -jnp.inf)
    far_keys = fetched_keys.reshape(DIST, blocks, BLK, HD)
    far_values = fetched_values.reshape(DIST, blocks, BLK, HD)
    query_blocks = queries.reshape(blocks, BLK, groups, HD)
    remote = (
        jnp.einsum("bqgd,jbud->gjbqu", query_blocks, far_keys, preferred_element_type=jnp.float32)
        * scale
    )
    remote = jnp.where(usable[None, :, None, None, None], remote, -jnp.inf)
    highest = jnp.maximum(local.max(-1), remote.max(axis=(1, 4)).reshape(groups, length))
    near_weight = jnp.exp(local - highest[:, :, None])
    far_weight = jnp.exp(remote - highest.reshape(groups, blocks, BLK)[:, None, :, :, None])
    denominator = near_weight.sum(-1) + far_weight.sum(axis=(1, 4)).reshape(groups, length)
    mixed = jnp.einsum(
        "gtu,ud->tgd", near_weight.astype(jnp.bfloat16), values, preferred_element_type=jnp.float32
    )
    far_mixed = jnp.einsum(
        "gjbqu,jbud->bqgd",
        far_weight.astype(jnp.bfloat16),
        far_values,
        preferred_element_type=jnp.float32,
    )
    mixed = mixed + far_mixed.reshape(length, groups, HD)
    attention = (
        (mixed / jnp.transpose(denominator)[:, :, None])
        .astype(jnp.bfloat16)
        .reshape(length, groups * HD)
    )
    near = bits_of("head")
    heads = lax.axis_size("head")
    turned_rows = jnp.concatenate(
        [
            lax.dynamic_slice_in_dim(
                attention, (lax.axis_index("head") ^ block) * residual.shape[0], residual.shape[0], 0
            )
            for block in range(heads)
        ]
    )
    pieces = jnp.dot(turned_rows, out_weight, preferred_element_type=jnp.float32).astype(
        jnp.bfloat16
    )
    pieces = pieces.reshape([2] * len(near) + list(residual.shape))
    summed = halve_all(pieces, near[::-1], near)
    attended = (residual.astype(jnp.float32) + summed.astype(jnp.float32)).astype(jnp.bfloat16)
    widened = attended.astype(jnp.float32)
    inverse = lax.rsqrt(jnp.mean(widened * widened, axis=-1, keepdims=True) + 1e-06)
    normed = (widened * inverse * norm_gain).astype(jnp.bfloat16)
    local_rows = normed.shape[0]
    width = normed.shape[1]
    devices = lax.axis_size(("ctx", "head"))
    experts = devices * EXP_DEV
    capacity = max(2, 2 * local_rows * TOP // experts)
    if devices * local_rows <= 2 * experts * capacity:
        moe_out = dense_experts(
            normed, expert_gate_up, expert_down, routes, route_weights, capacity
        )
    else:
        moe_out = routed_experts(
            normed, expert_gate_up, expert_down, routes, route_weights, capacity
        )
    return (attended, moe_out)


def solution(mesh):
    return jax.shard_map(
        body,
        mesh=mesh,
        in_specs=(
            P("ctx", "head"),
            P("ctx", "head"),
            P("ctx", "head"),
            P("head", None),
            P("head", None),
            P(("ctx", "head"), None),
            P(),
            P(("ctx", "head"), None, None),
            P(("ctx", "head"), None, None),
            P(("ctx", "head"), None),
            P(("ctx", "head"), None),
        ),
        out_specs=(P(("ctx", "head"), None), P(("ctx", "head"), None)),
        check_vma=False,
    )
```

```python
import math

import jax
import jax.numpy as jnp
from jax import lax
from jax.sharding import PartitionSpec as P

HD = 128
FFE = 768
TOP = 8
EXP_DEV = 1
BLK = 128
DIST = 3


def expert_rows(arrived, expert_gate_up, expert_down, sources):
    width = arrived.shape[2]
    grid = arrived.reshape(sources, EXP_DEV, arrived.shape[1], width)
    projected = jnp.einsum(
        "sekd,edf->eskf", grid, expert_gate_up, preferred_element_type=jnp.float32
    )
    hidden = (jax.nn.silu(projected[..., :FFE]) * projected[..., FFE:]).astype(jnp.bfloat16)
    output = jnp.einsum("eskf,efd->sekd", hidden, expert_down, preferred_element_type=jnp.float32)
    return output.astype(jnp.bfloat16).reshape(arrived.shape)


def bits_of(axis):
    return [(axis, 1 << at) for at in range(lax.axis_size(axis).bit_length() - 1)]


def swapped(array, axis, bit):
    return lax.ppermute(array, axis, [(i, i ^ bit) for i in range(lax.axis_size(axis))])


def double_all(array, order):
    for axis, bit in order:
        array = jnp.stack([array, swapped(array, axis, bit)])
    return array


def add(kept, got):
    return (kept.astype(jnp.float32) + got.astype(jnp.float32)).astype(jnp.bfloat16)


def halve_all(total, names, order):
    names = list(names)
    for axis, bit in order:
        dim = names.index((axis, bit))
        sent = lax.index_in_dim(total, 1, dim, keepdims=False)
        kept = lax.index_in_dim(total, 0, dim, keepdims=False)
        total = add(kept, swapped(sent, axis, bit))
        names.pop(dim)
    return total


def routed_experts(normed, expert_gate_up, expert_down, routes, route_weights, capacity):
    local_rows, width = normed.shape
    devices = lax.axis_size(("ctx", "head"))
    experts = devices * EXP_DEV
    flat_experts = routes.reshape(local_rows * TOP)
    onehot = (flat_experts[:, None] == jnp.arange(experts, dtype=jnp.int32)[None, :]).astype(
        jnp.int32
    )
    places = jnp.sum(jnp.cumsum(onehot, axis=0) * onehot, axis=1) - 1
    owners = jnp.arange(local_rows * TOP, dtype=jnp.int32) // TOP
    outgoing = (
        jnp.zeros((experts, capacity, width), jnp.bfloat16)
        .at[flat_experts, places]
        .set(normed[owners])
    )
    answered = expert_rows(
        lax.all_to_all(outgoing, ("ctx", "head"), split_axis=0, concat_axis=0, tiled=True),
        expert_gate_up,
        expert_down,
        devices,
    )
    returned = lax.all_to_all(answered, ("ctx", "head"), split_axis=0, concat_axis=0, tiled=True)
    picked = returned[flat_experts, places].astype(jnp.float32)
    weighted = route_weights.reshape(local_rows * TOP)[:, None] * picked
    moe_out = weighted.reshape(local_rows, TOP, width).sum(axis=1).astype(jnp.bfloat16)
    return moe_out


def dense_experts(normed, expert_gate_up, expert_down, routes, route_weights, capacity):
    local_rows, width = normed.shape
    near, far = bits_of("head"), bits_of("ctx")
    names = far[::-1] + near[::-1]
    core = names[-1]
    rest = names[:-1]
    straight, crossed = far[:1] + near[1:] + far[1:], near[1:] + far
    orders = (straight, crossed, far[1:] + far[:1] + near[1:], straight, crossed)
    delays = (0, 0, 0, 1, 1)
    widths = [share * width // 16 for share in (4, 4, 4, 2, 2)]
    starts = [sum(widths[:number]) for number in range(len(widths))]
    chunks = range(len(widths))
    steps = len(rest) + max(delays)
    shape = [2] * len(rest)
    half = 2 ** len(rest)
    table = double_all(
        jnp.concatenate([routes.astype(jnp.float32), route_weights], axis=1),
        rest[::-1] + [core],
    ).reshape(2 * half, local_rows, 2 * TOP)
    mine = lax.axis_index(("ctx", "head")).astype(jnp.float32)
    chosen = table[:, :, :TOP] == mine
    weight = jnp.sum(jnp.where(chosen, table[:, :, TOP:], 0.0), axis=2)
    named = jnp.any(chosen, axis=2)
    earlier = jnp.arange(local_rows)[:, None] < jnp.arange(local_rows)[None, :]
    places = jnp.dot(
        named.astype(jnp.bfloat16), earlier.astype(jnp.bfloat16), preferred_element_type=jnp.float32
    ).astype(jnp.int32)
    select = (
        named[:, None, :] & (places[:, None, :] == jnp.arange(capacity, dtype=jnp.int32)[None, :, None])
    ).astype(jnp.bfloat16)
    select = select.reshape(2, half, capacity, local_rows)
    weight = weight.reshape(2, half, local_rows)
    held = [normed[:, starts[n] : starts[n] + widths[n]] for n in chunks]
    for step in range(steps)[::-1]:
        active = [n for n in chunks if 0 <= step - delays[n] < len(rest)]
        if step < steps - 1:
            for n, array in zip(active, lax.optimization_barrier([held[n] for n in active])):
                held[n] = array
        for n in active:
            held[n] = double_all(held[n], [orders[n][step - delays[n]]])
    picked = ([], [])
    for n in chunks:
        for side, blocks in enumerate((held[n], swapped(held[n], *core))):
            blocks = jnp.transpose(
                blocks, [orders[n].index(name) for name in rest] + [len(rest), len(rest) + 1]
            ).reshape(half, local_rows, widths[n])
            picked[side].append(
                jnp.einsum(
                    "sct,std->scd", select[side], blocks, preferred_element_type=jnp.float32
                ).astype(jnp.bfloat16)
            )
    hidden = []
    for side in range(2):
        rows = jnp.concatenate(picked[side], axis=2).reshape(half * capacity, width)
        projected = jnp.dot(rows, expert_gate_up[0], preferred_element_type=jnp.float32)
        hidden.append((jax.nn.silu(projected[:, :FFE]) * projected[:, FFE:]).astype(jnp.bfloat16))
    totals = []
    for n in chunks:
        columns = slice(starts[n], starts[n] + widths[n])
        partial = []
        for side in range(2):
            output = jnp.dot(
                hidden[side], expert_down[0, :, columns], preferred_element_type=jnp.float32
            ).astype(jnp.bfloat16)
            spread = jnp.einsum(
                "sct,scd->std",
                select[side],
                output.reshape(half, capacity, widths[n]),
                preferred_element_type=jnp.float32,
            )
            partial.append((weight[side][:, :, None] * spread).astype(jnp.bfloat16))
        total = add(partial[0], swapped(partial[1], *core))
        totals.append(total.reshape(shape + [local_rows, widths[n]]))
    left = [list(rest) for n in chunks]
    for step in range(steps):
        active = [n for n in chunks if 0 <= step - delays[n] < len(rest)]
        if step:
            for n, array in zip(active, lax.optimization_barrier([totals[n] for n in active])):
                totals[n] = array
        for n in active:
            name = orders[n][step - delays[n]]
            totals[n] = halve_all(totals[n], left[n], [name])
            left[n].remove(name)
    return jnp.concatenate(totals, axis=1)


def body(
    queries,
    keys,
    values,
    distances,
    out_weight,
    residual,
    norm_gain,
    expert_gate_up,
    expert_down,
    routes,
    route_weights,
):
    length = queries.shape[0]
    groups = queries.shape[1] // HD
    blocks = length // BLK
    scale = 1.0 / math.sqrt(HD)
    wanted = distances[0]
    source = lax.axis_index("ctx") - wanted
    usable = source >= 0
    far = bits_of("ctx")
    every_key = double_all(keys, far[::-1]).reshape(-1, HD)
    every_value = double_all(values, far[:1] + far[:0:-1]).reshape(-1, HD)
    apart = jnp.maximum(source, 0) ^ lax.axis_index("ctx")
    shards = lax.axis_size("ctx")
    turned = sum(
        ((apart // bit) % 2) * (shards // 2 // bit) for axis, bit in far
    )
    key_offsets = turned * length
    value_bits = far[1:][::1] + far[:1]
    value_offsets = length * sum(
        ((apart // bit) % 2) * (shards >> (place + 1)) for place, (axis, bit) in enumerate(value_bits)
    )
    fetched_keys = jnp.stack(
        [
            lax.dynamic_slice_in_dim(every_key, key_offsets[slot_index], length, 0)
            for slot_index in range(DIST)
        ]
    )
    fetched_values = jnp.stack(
        [
            lax.dynamic_slice_in_dim(every_value, value_offsets[slot_index], length, 0)
            for slot_index in range(DIST)
        ]
    )
    query = queries.reshape(length, groups, HD)
    causal = jnp.arange(length)[:, None] >= jnp.arange(length)[None, :]
    local = jnp.einsum("tgd,ud->gtu", query, keys, preferred_element_type=jnp.float32) * scale
    local = jnp.where(causal[None], local, -jnp.inf)
    far_keys = fetched_keys.reshape(DIST, blocks, BLK, HD)
    far_values = fetched_values.reshape(DIST, blocks, BLK, HD)
    query_blocks = queries.reshape(blocks, BLK, groups, HD)
    remote = (
        jnp.einsum("bqgd,jbud->gjbqu", query_blocks, far_keys, preferred_element_type=jnp.float32)
        * scale
    )
    remote = jnp.where(usable[None, :, None, None, None], remote, -jnp.inf)
    highest = jnp.maximum(local.max(-1), remote.max(axis=(1, 4)).reshape(groups, length))
    near_weight = jnp.exp(local - highest[:, :, None])
    far_weight = jnp.exp(remote - highest.reshape(groups, blocks, BLK)[:, None, :, :, None])
    denominator = near_weight.sum(-1) + far_weight.sum(axis=(1, 4)).reshape(groups, length)
    mixed = jnp.einsum(
        "gtu,ud->tgd", near_weight.astype(jnp.bfloat16), values, preferred_element_type=jnp.float32
    )
    far_mixed = jnp.einsum(
        "gjbqu,jbud->bqgd",
        far_weight.astype(jnp.bfloat16),
        far_values,
        preferred_element_type=jnp.float32,
    )
    mixed = mixed + far_mixed.reshape(length, groups, HD)
    attention = (
        (mixed / jnp.transpose(denominator)[:, :, None])
        .astype(jnp.bfloat16)
        .reshape(length, groups * HD)
    )
    near = bits_of("head")
    heads = lax.axis_size("head")
    turned_rows = jnp.concatenate(
        [
            lax.dynamic_slice_in_dim(
                attention, (lax.axis_index("head") ^ block) * residual.shape[0], residual.shape[0], 0
            )
            for block in range(heads)
        ]
    )
    pieces = jnp.dot(turned_rows, out_weight, preferred_element_type=jnp.float32).astype(
        jnp.bfloat16
    )
    pieces = pieces.reshape([2] * len(near) + list(residual.shape))
    summed = halve_all(pieces, near[::-1], near)
    attended = (residual.astype(jnp.float32) + summed.astype(jnp.float32)).astype(jnp.bfloat16)
    widened = attended.astype(jnp.float32)
    inverse = lax.rsqrt(jnp.mean(widened * widened, axis=-1, keepdims=True) + 1e-06)
    normed = (widened * inverse * norm_gain).astype(jnp.bfloat16)
    local_rows = normed.shape[0]
    width = normed.shape[1]
    devices = lax.axis_size(("ctx", "head"))
    experts = devices * EXP_DEV
    capacity = max(2, 2 * local_rows * TOP // experts)
    if devices * local_rows <= 2 * experts * capacity:
        moe_out = dense_experts(
            normed, expert_gate_up, expert_down, routes, route_weights, capacity
        )
    else:
        moe_out = routed_experts(
            normed, expert_gate_up, expert_down, routes, route_weights, capacity
        )
    return (attended, moe_out)


def solution(mesh):
    return jax.shard_map(
        body,
        mesh=mesh,
        in_specs=(
            P("ctx", "head"),
            P("ctx", "head"),
            P("ctx", "head"),
            P("head", None),
            P("head", None),
            P(("ctx", "head"), None),
            P(),
            P(("ctx", "head"), None, None),
            P(("ctx", "head"), None, None),
            P(("ctx", "head"), None),
            P(("ctx", "head"), None),
        ),
        out_specs=(P(("ctx", "head"), None), P(("ctx", "head"), None)),
        check_vma=False,
    )
```
